32 devices in a mesh: section: 4 (over x, core), tp: 8 (over z, y).
Axes of the slice: x: 2, y: 2, z: 4, core: 2. Of those that a mesh axis runs over, the one named last changes fastest.
Arguments:
- layer_inputs: bfloat16 [8, 512, 4096], P('section', None, 'tp'), may hold values from -6 to 6
- weights: bfloat16 [8, 4096, 4096], P('section', 'tp'), may hold values from -0.046875 to 0.046875
- input_basis: bfloat16 [8, 4096, 64], P('section', 'tp'), may hold values from -0.09375 to 0.09375
- output_basis: bfloat16 [8, 4096, 32], P('section', 'tp'), may hold values from -0.09375 to 0.09375
- queries: bfloat16 [8, 512, 2048], P('section', 'tp'), may hold values from -0.00390625 to 0.00390625
- top_cotangent: bfloat16 [512, 4096], replicated, may hold values from -6 to 6
- sequence_example: int32 [4], replicated, may hold values from 0 to 1
Outputs:
- scores: float32 [2, 512], P(None, 'tp')
The draws below stay inside these ranges and needn't reach their ends.
All inputs are finite; a program needn't handle non-finite values.
Results may differ from the reference program's by a relative error of at most 0.0094.
Values may be sent and summed in bfloat16 or wider, within the bound.
A program may use at most 64 MiB of HBM per device.

```python
import jax
import jax.numpy as jnp
from jax import lax

D = 4096
RIN = 64
ROUT = 32
NQ = 512
SEQLEN = 128
LAYERS = 8
KDIM = 2048
SEQS = 4
TOKENS = 512
EXAMPLES = 2


def set_ends(values, stream_key, low, high):
    shape = values.shape
    spot = [jax.random.randint(jax.random.fold_in(stream_key, axis), (), 0, shape[axis]) for axis in range(len(shape))]
    values = values.at[tuple(spot)].set(low)
    longest = shape.index(max(shape))
    spot[longest] = (spot[longest] + 1) % shape[longest]
    return values.at[tuple(spot)].set(high)


def block_scale(own_key, extent, split, least, top_value):
    def one(axis_at, parts):
        steps = jax.random.uniform(jax.random.fold_in(jax.random.fold_in(own_key, 6), axis_at), (parts,), jnp.float32, least / len(split), top_value / len(split))
        return jnp.repeat(jnp.exp(steps), extent[axis_at] // parts).reshape((-1,) + (1,) * (len(extent) - axis_at - 1))

    factor_of = one(*split[0])
    for cut in split[1:]:
        factor_of = factor_of * one(*cut)
    return factor_of


def scatter_about(key, shape, deviation, most, pieces=(), kind=jnp.bfloat16):
    drawn = jax.random.normal(key, shape, jnp.float32) * deviation
    if len(pieces) > 0:
        drawn = block_scale(key, shape, pieces, -0.22, 0.18) * drawn
    return jnp.clip(drawn, min=-most, max=most).astype(kind)


def setup_inputs(seed: int = 0) -> dict:
    streams_of = jax.random.split(jax.random.key(seed), 8)
    layer_inputs = scatter_about(streams_of[0], (LAYERS, TOKENS, D), 1.0, 6.0, ((0, 4), (2, 8)))
    weights = scatter_about(streams_of[1], (LAYERS, D, D), (4 * D) ** -0.5, 0.046875, ((0, 4), (1, 8)))
    input_basis = scatter_about(streams_of[2], (LAYERS, D, RIN), D ** -0.5, 0.09375, ((0, 4), (1, 8)))
    output_basis = scatter_about(streams_of[3], (LAYERS, D, ROUT), D ** -0.5, 0.09375, ((0, 4), (1, 8)))
    queries = scatter_about(streams_of[4], (LAYERS, NQ, KDIM), (KDIM * 1024) ** -0.5, 0.00390625, ((0, 4), (1, 8)))
    top_cotangent = scatter_about(streams_of[5], (TOKENS, D), 1.0, 6.0)
    sequence_example = set_ends(jax.random.randint(streams_of[6], (SEQS,), 0, EXAMPLES), jax.random.fold_in(streams_of[6], 1), 0, EXAMPLES - 1).astype(jnp.int32)
    return dict(layer_inputs=layer_inputs, weights=weights, input_basis=input_basis, output_basis=output_basis, queries=queries, top_cotangent=top_cotangent, sequence_example=sequence_example)


def reference(layer_inputs, weights, input_basis, output_basis, queries, top_cotangent, sequence_example):
    token_examples = jnp.repeat(sequence_example, SEQLEN)
    selector = (jnp.arange(EXAMPLES, dtype=jnp.int32)[:, None] == token_examples[None, :]).astype(jnp.float32)

    def layer_step(cotangent, inputs):
        hidden, matrix, basis_in, basis_out, stored_queries = inputs
        floats = hidden.astype(jnp.float32)
        logistic = jax.nn.sigmoid(floats)
        activated = (floats * logistic).astype(jnp.bfloat16)
        slope = logistic * (1.0 + floats * (1.0 - logistic))
        in_feats = jnp.dot(activated, basis_in, preferred_element_type=jnp.float32)
        out_feats = jnp.dot(cotangent, basis_out, preferred_element_type=jnp.float32)
        joined = (out_feats[:, :, None] * in_feats[:, None, :]).reshape(out_feats.shape[0], -1)
        grads = jnp.dot(selector, joined, precision=lax.Precision.HIGHEST)
        layer_scores = jnp.dot(grads, stored_queries.astype(jnp.float32).T, precision=lax.Precision.HIGHEST)
        branch = jnp.dot(cotangent, matrix.T, preferred_element_type=jnp.float32)
        updated = (cotangent.astype(jnp.float32) + slope * branch).astype(jnp.bfloat16)
        return updated, layer_scores

    final, stacked = lax.scan(layer_step, top_cotangent, (layer_inputs, weights, input_basis, output_basis, queries), reverse=True)
    return jnp.sum(stacked, axis=0)
```

```python
import functools

import jax
import jax.numpy as jnp
from jax import lax
from jax.experimental import pallas as pl
from jax.experimental.pallas import tpu as pltpu
from jax.sharding import PartitionSpec as P

EXAMPLES = 2
MICRO = 8
MESH = pl.DeviceIdType.MESH
NT = (((1,), (1,)), ((), ()))


def grid_of(tp_count):
    ny = 1
    while (2 * ny) * (2 * ny) <= tp_count:
        ny *= 2
    return tp_count // ny, ny


def slope_of(hidden):
    floats = hidden.astype(jnp.float32)
    logistic = jax.nn.sigmoid(floats)
    return logistic * (1.0 + floats * (1.0 - logistic))


def chain_kernel(
    sections, tp_count, top_ref, w_ref, h_ref, ob_ref, po_ref,
    buf_u, buf_m, buf_l, w_v,
    w_sem, recv_u, recv_m, send_m, send_my, relay_u, relay_m, send_l,
):
    nz, ny = grid_of(tp_count)
    sec = lax.axis_index("section")
    tp = lax.axis_index("tp")
    z, y = tp // ny, lax.rem(tp, ny)
    micro, _, rows, width = buf_u.shape
    is_top = sec == sections - 1
    has_lower = sec > 0

    def peer_z(step):
        return lax.rem(z + step, nz) * ny + y

    def peer_y(step):
        return z * ny + lax.rem(y + step, ny)

    def src_at(zstep, ystep):
        return lax.rem(z + zstep, nz) * ny + lax.rem(y + ystep, ny)

    def w_copy(layer):
        return pltpu.make_async_copy(w_ref.at[layer], w_v.at[layer], w_sem.at[layer])

    def top_copy(m, k):
        return pltpu.make_async_copy(
            top_ref.at[pl.ds(pl.multiple_of(m * rows, rows), rows), pl.ds(k * width, width)],
            buf_u.at[m, k], recv_u.at[m, k])

    def remote(src, dst, ssem, rsem, to_sec, to_tp):
        return pltpu.make_async_remote_copy(
            src_ref=src, dst_ref=dst, send_sem=ssem, recv_sem=rsem,
            device_id=(to_sec, to_tp), device_id_type=MESH)

    @pl.when(is_top)
    def _():
        @pl.loop(0, micro)
        def _(m):
            for k in range(tp_count):
                top_copy(m, k).start()

    w_copy(1).start()
    w_copy(0).start()

    barrier = pltpu.get_barrier_semaphore()
    for step in range(1, nz):
        pl.semaphore_signal(barrier, inc=1, device_id=(sec, peer_z(step)), device_id_type=MESH)
    for step in range(1, ny):
        pl.semaphore_signal(barrier, inc=1, device_id=(sec, peer_y(step)), device_id_type=MESH)

    @pl.when(has_lower)
    def _():
        for step in range(nz):
            pl.semaphore_signal(
                barrier, inc=1, device_id=(sec - 1, peer_z(step)), device_id_type=MESH)

    @pl.when(jnp.logical_not(is_top))
    def _():
        for step in range(nz):
            pl.semaphore_signal(
                barrier, inc=1, device_id=(sec + 1, peer_z(step)), device_id_type=MESH)

    linked = has_lower.astype(jnp.int32) + jnp.logical_not(is_top).astype(jnp.int32)
    pl.semaphore_wait(barrier, nz + ny - 2 + nz * linked)

    def relay_u_copy(m, zstep, ystep):
        src = src_at(zstep, 0)
        return remote(buf_u.at[m, src], buf_u.at[m, src], relay_u.at[m, zstep, ystep],
                      recv_u.at[m, src], sec, peer_y(ystep))

    def relay_m_copy(m, zstep, ystep):
        src = src_at(zstep, 0)
        return remote(buf_m.at[m, src], buf_m.at[m, src], relay_m.at[m, zstep, ystep],
                      recv_m.at[m, src], sec, peer_y(ystep))

    def middle_copy(m, zstep):
        return remote(buf_m.at[m, tp], buf_m.at[m, tp], send_m.at[m, zstep],
                      recv_m.at[m, tp], sec, peer_z(zstep))

    def lower_copy(m, zstep):
        return remote(buf_l.at[m], buf_u.at[m, tp], send_l.at[m, zstep],
                      recv_u.at[m, tp], sec - 1, peer_z(zstep))

    def await_u(m, src):
        remote(buf_u.at[m, src], buf_u.at[m, src], send_my, recv_u.at[m, src], sec, tp).wait_recv()

    def await_m(m, src):
        remote(buf_m.at[m, src], buf_m.at[m, src], send_my, recv_m.at[m, src], sec, tp).wait_recv()

    def product(buf, m, layer):
        total = None
        for k in range(tp_count):
            term = lax.dot_general(
                buf[m, k], w_v[layer, :, k * width:(k + 1) * width], NT,
                preferred_element_type=jnp.float32)
            total = term if total is None else total + term
        return total

    def upper(m):
        at = pl.ds(pl.multiple_of(m * rows, rows), rows)
        own = buf_u[m, tp]
        floats = own.astype(jnp.float32)
        middle = (floats + slope_of(h_ref[1, at, :]) * product(buf_u, m, 1)).astype(jnp.bfloat16)
        buf_m[m, tp] = middle

        @pl.when(has_lower)
        def _():
            for step in range(1, nz):
                middle_copy(m, step).start()
            for step in range(1, ny):
                relay_m_copy(m, 0, step).start()

        po_ref[1, at, :] = jnp.dot(own, ob_ref[1], preferred_element_type=jnp.float32)
        po_ref[0, at, :] = jnp.dot(middle, ob_ref[0], preferred_element_type=jnp.float32)

    def lower(m):
        at = pl.ds(pl.multiple_of(m * rows, rows), rows)
        floats = buf_m[m, tp].astype(jnp.float32)
        buf_l[m] = (floats + slope_of(h_ref[0, at, :]) * product(buf_m, m, 0)).astype(jnp.bfloat16)
        for step in range(nz):
            lower_copy(m, step).start()

    @pl.loop(0, micro + 1)
    def _(it):
        @pl.when(jnp.logical_and(it < micro, jnp.logical_not(is_top)))
        def _():
            for zstep in range(nz):
                await_u(it, src_at(zstep, 0))
                for ystep in range(1, ny):
                    relay_u_copy(it, zstep, ystep).start()

        @pl.when(it == 0)
        def _():
            w_copy(1).wait()

        @pl.when(it == 1)
        def _():
            w_copy(0).wait()

        @pl.when(it < micro)
        def _():
            @pl.when(is_top)
            def _():
                for k in range(tp_count):
                    top_copy(it, k).wait()

            @pl.when(jnp.logical_not(is_top))
            def _():
                for zstep in range(nz):
                    for ystep in range(1, ny):
                        await_u(it, src_at(zstep, ystep))

            upper(it)

        @pl.when(jnp.logical_and(it >= 1, has_lower))
        def _():
            m = it - 1
            for zstep in range(1, nz):
                await_m(m, src_at(zstep, 0))
                for ystep in range(1, ny):
                    relay_m_copy(m, zstep, ystep).start()
            for zstep in range(nz):
                for ystep in range(1, ny):
                    await_m(m, src_at(zstep, ystep))
            lower(m)

    @pl.loop(0, micro)
    def _(m):
        @pl.when(jnp.logical_not(is_top))
        def _():
            for zstep in range(nz):
                for ystep in range(1, ny):
                    relay_u_copy(m, zstep, ystep).wait_send()

        @pl.when(has_lower)
        def _():
            for zstep in range(1, nz):
                middle_copy(m, zstep).wait_send()
            for zstep in range(nz):
                for ystep in range(1, ny):
                    relay_m_copy(m, zstep, ystep).wait_send()
                lower_copy(m, zstep).wait_send()


def chain(sections, tp_count, top, weights, hidden, output_basis):
    tokens = top.shape[0]
    width = hidden.shape[2]
    rows = tokens // MICRO
    nz, ny = grid_of(tp_count)
    dma = pltpu.SemaphoreType.DMA
    vmem = pl.BlockSpec(memory_space=pltpu.VMEM)
    hbm = pl.BlockSpec(memory_space=pl.ANY)
    return pl.pallas_call(
        functools.partial(chain_kernel, sections, tp_count),
        out_shape=jax.ShapeDtypeStruct((2, tokens, output_basis.shape[2]), jnp.float32),
        in_specs=[hbm, hbm, vmem, vmem],
        out_specs=vmem,
        scratch_shapes=[
            pltpu.VMEM((MICRO, tp_count, rows, width), jnp.bfloat16),
            pltpu.VMEM((MICRO, tp_count, rows, width), jnp.bfloat16),
            pltpu.VMEM((MICRO, rows, width), jnp.bfloat16),
            pltpu.VMEM(weights.shape, jnp.bfloat16),
            dma((2,)),
            dma((MICRO, tp_count)),
            dma((MICRO, tp_count)),
            dma((MICRO, nz)),
            dma,
            dma((MICRO, nz, ny)),
            dma((MICRO, nz, ny)),
            dma((MICRO, nz)),
        ],
        compiler_params=pltpu.CompilerParams(
            collective_id=0, has_side_effects=True, vmem_limit_bytes=56 * 2**20),
    )(top, weights, hidden, output_basis)


def shards(
    layer_inputs, weights, input_basis, output_basis, queries, top_cotangent, sequence_example
):
    sections = lax.axis_size("section")
    tp_count = lax.axis_size("tp")
    tokens = layer_inputs.shape[1]
    floats = layer_inputs.astype(jnp.float32)
    activated = (floats * jax.nn.sigmoid(floats)).astype(jnp.bfloat16)
    partial_in = jnp.einsum(
        "ltd,ldr->ltr", activated, input_basis, preferred_element_type=jnp.float32
    )
    in_feats = lax.psum(partial_in, "tp")
    out_feats = chain(sections, tp_count, top_cotangent, weights, layer_inputs, output_basis)
    token_example = jnp.repeat(sequence_example, tokens // sequence_example.shape[0])
    selector = (
        jnp.arange(EXAMPLES, dtype=jnp.int32)[:, None] == token_example[None, :]
    ).astype(jnp.float32)
    chosen = selector[None, :, :, None] * out_feats[:, None]
    partial = jnp.einsum("leto,lti->leoi", chosen, in_feats, precision=lax.Precision.HIGHEST)
    grads = lax.psum(partial.reshape(2, EXAMPLES, -1), "tp")
    layer_scores = jnp.einsum(
        "lek,lqk->eq", grads, queries.astype(jnp.float32), precision=lax.Precision.HIGHEST
    )
    return lax.psum(layer_scores, "section")


def solution(mesh):
    placed = (
        P("section", None, "tp"),
        P("section", "tp", None),
        P("section", "tp", None),
        P("section", "tp", None),
        P("section", "tp", None),
        P(),
        P(),
    )
    return jax.shard_map(
        shards, mesh=mesh, in_specs=placed, out_specs=P(None, "tp"), check_vma=False
    )
```

```python
import functools

import jax
import jax.numpy as jnp
from jax import lax
from jax.experimental import pallas as pl
from jax.experimental.pallas import tpu as pltpu
from jax.sharding import PartitionSpec as P

EXAMPLES = 2
MESH = pl.DeviceIdType.MESH
NT = (((1,), (1,)), ((), ()))


def grid_of(tp_count):
    ny = 1
    while (2 * ny) * (2 * ny) <= tp_count:
        ny *= 2
    return tp_count // ny, ny


def slope_of(hidden):
    floats = hidden.astype(jnp.float32)
    logistic = jax.nn.sigmoid(floats)
    return logistic * (1.0 + floats * (1.0 - logistic))


def chain_kernel(
    sections, tp_count, top_ref, w_ref, h_ref, ib_ref, ob_ref, q_ref, se_ref, score_ref,
    buf_u, buf_m, buf_l, w_v, ob_v, ib_v, out_v, part_in, got_in, full_in, grad_v, sum_v, score_v,
    w_sem, recv_u, recv_m, send_m, send_my, relay_u, relay_m, send_l,
    part_send, part_recv, full_send, full_recv, grad_send, grad_recv, score_send, score_recv,
):
    nz, ny = grid_of(tp_count)
    sec = lax.axis_index("section")
    tp = lax.axis_index("tp")
    z, y = tp // ny, lax.rem(tp, ny)
    micro, _, rows, width = buf_u.shape
    is_top = sec == sections - 1
    has_lower = sec > 0

    def peer_z(step):
        return lax.rem(z + step, nz) * ny + y

    def peer_y(step):
        return z * ny + lax.rem(y + step, ny)

    def src_at(zstep, ystep):
        return lax.rem(z + zstep, nz) * ny + lax.rem(y + ystep, ny)

    def w_copy(layer):
        return pltpu.make_async_copy(w_ref.at[layer], w_v.at[layer], w_sem.at[layer])

    def top_copy(m, k):
        return pltpu.make_async_copy(
            top_ref.at[pl.ds(pl.multiple_of(m * rows, rows), rows), pl.ds(k * width, width)],
            buf_u.at[m, k], recv_u.at[m, k])

    def remote(src, dst, ssem, rsem, to_sec, to_tp):
        return pltpu.make_async_remote_copy(
            src_ref=src, dst_ref=dst, send_sem=ssem, recv_sem=rsem,
            device_id=(to_sec, to_tp), device_id_type=MESH)

    rank_in, rank_out = ib_ref.shape[2], ob_ref.shape[2]

    def prepare_bases():
        gap_in = jnp.zeros((width, rank_in), jnp.float32)
        gap_out = jnp.zeros((width, EXAMPLES * rank_out), jnp.float32)
        for layer in range(2):
            basis_in = ib_ref[layer].astype(jnp.float32)
            basis_out = [ob_ref[layer].astype(jnp.float32)] * EXAMPLES
            ins = [basis_in, gap_in] if layer == 0 else [gap_in, basis_in]
            outs = basis_out + [gap_out] if layer == 0 else [gap_out] + basis_out
            ib_v[layer] = jnp.concatenate(ins, 1).astype(jnp.bfloat16)
            ob_v[layer] = jnp.concatenate(outs, 1).astype(jnp.bfloat16)

    @pl.when(is_top)
    def _():
        @pl.loop(0, micro)
        def _(m):
            for k in range(tp_count):
                top_copy(m, k).start()

    w_copy(1).start()
    w_copy(0).start()

    barrier = pltpu.get_barrier_semaphore()

    def greet(to_sec, to_tp):
        pl.semaphore_signal(barrier, inc=1, device_id=(to_sec, to_tp), device_id_type=MESH)

    for step in range(1, tp_count):
        greet(sec, lax.rem(tp + step, tp_count))

    @pl.when(has_lower)
    def _():
        for step in range(nz):
            greet(sec - 1, peer_z(step))

    @pl.when(jnp.logical_not(is_top))
    def _():
        for step in range(nz):
            greet(sec + 1, peer_z(step))

    for step in range(1, sections):
        other = lax.rem(sec + step, sections)

        @pl.when(jnp.logical_and(other != sec + 1, other != sec - 1))
        def _(other=other):
            greet(other, tp)

    prepare_bases()
    linked = has_lower.astype(jnp.int32) + jnp.logical_not(is_top).astype(jnp.int32)
    pl.semaphore_wait(barrier, tp_count + sections - 2 + (nz - 1) * linked)

    def relay_u_copy(m, zstep, ystep):
        src = src_at(zstep, 0)
        return remote(buf_u.at[m, src], buf_u.at[m, src], relay_u.at[m, zstep, ystep],
                      recv_u.at[m, src], sec, peer_y(ystep))

    def relay_m_copy(m, zstep, ystep):
        src = src_at(zstep, 0)
        return remote(buf_m.at[m, src], buf_m.at[m, src], relay_m.at[m, zstep, ystep],
                      recv_m.at[m, src], sec, peer_y(ystep))

    def middle_copy(m, zstep):
        return remote(buf_m.at[m, tp], buf_m.at[m, tp], send_m.at[m, zstep],
                      recv_m.at[m, tp], sec, peer_z(zstep))

    def lower_copy(m, zstep):
        return remote(buf_l.at[m], buf_u.at[m, tp], send_l.at[m, zstep],
                      recv_u.at[m, tp], sec - 1, peer_z(zstep))

    def await_u(m, src):
        remote(buf_u.at[m, src], buf_u.at[m, src], send_my, recv_u.at[m, src], sec, tp).wait_recv()

    def await_m(m, src):
        remote(buf_m.at[m, src], buf_m.at[m, src], send_my, recv_m.at[m, src], sec, tp).wait_recv()

    def product(buf, m, layer):
        total = None
        for k in range(tp_count):
            term = lax.dot_general(
                buf[m, k], w_v[layer, :, k * width:(k + 1) * width], NT,
                preferred_element_type=jnp.float32)
            total = term if total is None else total + term
        return total

    def upper(m):
        at = pl.ds(pl.multiple_of(m * rows, rows), rows)
        own = buf_u[m, tp]
        floats = own.astype(jnp.float32)
        middle = (floats + slope_of(h_ref[1, at, :]) * product(buf_u, m, 1)).astype(jnp.bfloat16)
        buf_m[m, tp] = middle

        @pl.when(has_lower)
        def _():
            for step in range(1, nz):
                middle_copy(m, step).start()
            for step in range(1, ny):
                relay_m_copy(m, 0, step).start()

        feats = jnp.dot(own, ob_v[1], preferred_element_type=jnp.float32) + jnp.dot(
            middle, ob_v[0], preferred_element_type=jnp.float32)
        example = se_ref[m * rows // (micro * rows // se_ref.shape[0])]
        lane_example = lax.rem(
            lax.broadcasted_iota(jnp.int32, feats.shape, 1) // rank_out, EXAMPLES)
        out_v[at, :] = jnp.where(lane_example == example, feats, 0.0)

    def lower(m):
        at = pl.ds(pl.multiple_of(m * rows, rows), rows)
        floats = buf_m[m, tp].astype(jnp.float32)
        buf_l[m] = (floats + slope_of(h_ref[0, at, :]) * product(buf_m, m, 0)).astype(jnp.bfloat16)
        for step in range(nz):
            lower_copy(m, step).start()

    def tp_copy(src, dst, ssem, rsem, to_tp):
        return remote(src, dst, ssem, rsem, sec, to_tp)

    def part_copy(step):
        to = lax.rem(tp + step, tp_count)
        return tp_copy(part_in.at[to], got_in.at[tp], part_send.at[step], part_recv.at[tp], to)

    def full_copy(step):
        to = lax.rem(tp + step, tp_count)
        return tp_copy(full_in.at[tp], full_in.at[tp], full_send.at[step], full_recv.at[tp], to)

    def grad_copy(step):
        to = lax.rem(tp + step, tp_count)
        return tp_copy(grad_v.at[tp], grad_v.at[tp], grad_send.at[step], grad_recv.at[tp], to)

    def score_copy(step):
        to = lax.rem(sec + step, sections)
        return remote(score_v.at[sec], score_v.at[sec], score_send.at[step],
                      score_recv.at[sec], to, tp)

    def project_inputs():
        @pl.loop(0, tp_count)
        def _(k):
            at = pl.ds(pl.multiple_of(k * rows, rows), rows)
            total = None
            for layer in range(2):
                floats = h_ref[layer, at, :].astype(jnp.float32)
                activated = (floats * jax.nn.sigmoid(floats)).astype(jnp.bfloat16)
                term = jnp.dot(activated, ib_v[layer], preferred_element_type=jnp.float32)
                total = term if total is None else total + term
            part_in[k] = total

        for step in range(1, tp_count):
            part_copy(step).start()
        total = part_in[tp]
        for step in range(1, tp_count):
            src = lax.rem(tp + step, tp_count)
            tp_copy(got_in.at[src], got_in.at[src], send_my, part_recv.at[src], tp).wait_recv()
            total = total + got_in[src]
        full_in[tp] = total
        for step in range(1, tp_count):
            full_copy(step).start()

    @pl.when(jnp.logical_not(is_top))
    def _():
        project_inputs()

    def pass_middle(m):
        for zstep in range(1, nz):
            await_m(m, src_at(zstep, 0))
            for ystep in range(1, ny):
                relay_m_copy(m, zstep, ystep).start()

    @pl.loop(0, micro + 1)
    def _(it):
        with_middle = jnp.logical_and(it >= 1, has_lower)

        @pl.when(jnp.logical_and(it < micro, jnp.logical_not(is_top)))
        def _():
            for zstep in range(nz):
                await_u(it, src_at(zstep, 0))
                for ystep in range(1, ny):
                    relay_u_copy(it, zstep, ystep).start()

        @pl.when(jnp.logical_and(with_middle, jnp.logical_not(is_top)))
        def _():
            pass_middle(it - 1)

        @pl.when(it == 0)
        def _():
            w_copy(1).wait()

        @pl.when(it == 1)
        def _():
            w_copy(0).wait()

        @pl.when(it < micro)
        def _():
            @pl.when(is_top)
            def _():
                for k in range(tp_count):
                    top_copy(it, k).wait()

            @pl.when(jnp.logical_not(is_top))
            def _():
                for zstep in range(nz):
                    for ystep in range(1, ny):
                        await_u(it, src_at(zstep, ystep))

            upper(it)

        @pl.when(with_middle)
        def _():
            m = it - 1

            @pl.when(is_top)
            def _():
                pass_middle(m)

            for zstep in range(nz):
                for ystep in range(1, ny):
                    await_m(m, src_at(zstep, ystep))
            lower(m)

    @pl.when(is_top)
    def _():
        project_inputs()

    for step in range(1, tp_count):
        src = lax.rem(tp + step, tp_count)
        tp_copy(full_in.at[src], full_in.at[src], send_my, full_recv.at[src], tp).wait_recv()
    lanes = 2 * rank_in
    pairs = EXAMPLES * rank_out
    product_all = lax.dot_general(
        out_v[...], full_in[...].reshape(micro * rows, lanes), (((0,), (0,)), ((), ())),
        precision=lax.Precision.HIGHEST, preferred_element_type=jnp.float32)
    lane = lax.broadcasted_iota(jnp.int32, (pairs, lanes), 1)
    grad_v[tp] = jnp.where(lane < rank_in, product_all[:pairs], product_all[pairs:])
    for step in range(1, tp_count):
        grad_copy(step).start()
    for step in range(1, tp_count):
        src = lax.rem(tp + step, tp_count)
        tp_copy(grad_v.at[src], grad_v.at[src], send_my, grad_recv.at[src], tp).wait_recv()
    total = grad_v[0]
    for k in range(1, tp_count):
        total = total + grad_v[k]
    sum_v[...] = total
    half = rank_out // 2
    number = q_ref.shape[1]
    sums = []
    for example in range(EXAMPLES):
        even = sum_v[pl.ds(example * rank_out, half, stride=2), :]
        odd = sum_v[pl.ds(example * rank_out + 1, half, stride=2), :]
        acc = jnp.zeros((number, lanes), jnp.float32)
        for layer in range(2):
            part = slice(layer * rank_in, (layer + 1) * rank_in)
            tiles = jnp.concatenate([even[:, part], odd[:, part]], 1)
            for j in range(half):
                block = q_ref[layer, :, j * lanes:(j + 1) * lanes].astype(jnp.float32)
                acc = acc + tiles[j:j + 1, :] * block
        sums.append(acc)
    score_v[sec] = lax.dot_general(
        jnp.ones((8, lanes), jnp.float32), jnp.concatenate(sums, 0), NT,
        precision=lax.Precision.HIGHEST, preferred_element_type=jnp.float32)
    for step in range(1, sections):
        score_copy(step).start()
    for step in range(1, sections):
        src = lax.rem(sec + step, sections)
        remote(score_v.at[src], score_v.at[src], send_my, score_recv.at[src], sec, tp).wait_recv()
    total = score_v[0]
    for k in range(1, sections):
        total = total + score_v[k]
    for example in range(EXAMPLES):
        score_ref[example:example + 1, :] = total[0:1, example * number:(example + 1) * number]

    for step in range(1, tp_count):
        part_copy(step).wait_send()
        full_copy(step).wait_send()
        grad_copy(step).wait_send()
    for step in range(1, sections):
        score_copy(step).wait_send()

    @pl.loop(0, micro)
    def _(m):
        @pl.when(jnp.logical_not(is_top))
        def _():
            for zstep in range(nz):
                for ystep in range(1, ny):
                    relay_u_copy(m, zstep, ystep).wait_send()

        @pl.when(has_lower)
        def _():
            for zstep in range(1, nz):
                middle_copy(m, zstep).wait_send()
            for zstep in range(nz):
                for ystep in range(1, ny):
                    relay_m_copy(m, zstep, ystep).wait_send()
                lower_copy(m, zstep).wait_send()


def shards(
    layer_inputs, weights, input_basis, output_basis, queries, top_cotangent, sequence_example
):
    sections = lax.axis_size("section")
    tp_count = lax.axis_size("tp")
    tokens, width = layer_inputs.shape[1:]
    micro = tp_count
    rows = tokens // micro
    nz, ny = grid_of(tp_count)
    lanes = 2 * input_basis.shape[2]
    pairs = EXAMPLES * output_basis.shape[2]
    number = queries.shape[1]
    dma = pltpu.SemaphoreType.DMA
    vmem = pl.BlockSpec(memory_space=pltpu.VMEM)
    hbm = pl.BlockSpec(memory_space=pl.ANY)
    smem = pl.BlockSpec(memory_space=pltpu.SMEM)
    return pl.pallas_call(
        functools.partial(chain_kernel, sections, tp_count),
        out_shape=jax.ShapeDtypeStruct((EXAMPLES, number), jnp.float32),
        in_specs=[hbm, hbm, vmem, vmem, vmem, vmem, smem],
        out_specs=vmem,
        scratch_shapes=[
            pltpu.VMEM((micro, tp_count, rows, width), jnp.bfloat16),
            pltpu.VMEM((micro, tp_count, rows, width), jnp.bfloat16),
            pltpu.VMEM((micro, rows, width), jnp.bfloat16),
            pltpu.VMEM(weights.shape, jnp.bfloat16),
            pltpu.VMEM((2, width, 2 * pairs), jnp.bfloat16),
            pltpu.VMEM((2, width, lanes), jnp.bfloat16),
            pltpu.VMEM((tokens, 2 * pairs), jnp.float32),
            pltpu.VMEM((tp_count, rows, lanes), jnp.float32),
            pltpu.VMEM((tp_count, rows, lanes), jnp.float32),
            pltpu.VMEM((tp_count, rows, lanes), jnp.float32),
            pltpu.VMEM((tp_count, pairs, lanes), jnp.float32),
            pltpu.VMEM((pairs, lanes), jnp.float32),
            pltpu.VMEM((sections, 8, EXAMPLES * number), jnp.float32),
            dma((2,)),
            dma((micro, tp_count)),
            dma((micro, tp_count)),
            dma((micro, nz)),
            dma,
            dma((micro, nz, ny)),
            dma((micro, nz, ny)),
            dma((micro, nz)),
            dma((tp_count,)),
            dma((tp_count,)),
            dma((tp_count,)),
            dma((tp_count,)),
            dma((tp_count,)),
            dma((tp_count,)),
            dma((sections,)),
            dma((sections,)),
        ],
        compiler_params=pltpu.CompilerParams(
            collective_id=0, has_side_effects=True, vmem_limit_bytes=56 * 2**20),
    )(top_cotangent, weights, layer_inputs, input_basis, output_basis, queries, sequence_example)


def solution(mesh):
    placed = (
        P("section", None, "tp"),
        P("section", "tp", None),
        P("section", "tp", None),
        P("section", "tp", None),
        P("section", "tp", None),
        P(),
        P(),
    )
    return jax.shard_map(
        shards, mesh=mesh, in_specs=placed, out_specs=P(None, "tp"), check_vma=False
    )
```

```python
import functools

import jax
import jax.numpy as jnp
from jax import lax
from jax.experimental import pallas as pl
from jax.experimental.pallas import tpu as pltpu
from jax.sharding import PartitionSpec as P

EXAMPLES = 2
MESH = pl.DeviceIdType.MESH
NT = (((1,), (1,)), ((), ()))


def grid_of(tp_count):
    ny = 1
    while (2 * ny) * (2 * ny) <= tp_count:
        ny *= 2
    return tp_count // ny, ny


def slope_of(hidden):
    floats = hidden.astype(jnp.float32)
    logistic = jax.nn.sigmoid(floats)
    return logistic * (1.0 + floats * (1.0 - logistic))


def chain_kernel(
    sections, tp_count, top_ref, w_ref, h_ref, ib_ref, ob_ref, q_ref, se_ref, score_ref,
    buf_u, buf_m, buf_l, w_v, ob_v, ib_v, out_v, part_in, got_in, full_in, grad_v, sum_v, score_v,
    w_sem, recv_u, recv_m, send_m, send_my, relay_u, relay_m, send_l,
    part_send, part_recv, full_send, full_recv, grad_send, grad_recv, score_send, score_recv,
):
    nz, ny = grid_of(tp_count)
    sec = lax.axis_index("section")
    tp = lax.axis_index("tp")
    z, y = tp // ny, lax.rem(tp, ny)
    micro, _, rows, width = buf_u.shape
    is_top = sec == sections - 1
    has_lower = sec > 0

    far = [z]
    for k in range(nz - 1):
        down = nz - 1 - k
        from_low = down - (z >= down).astype(jnp.int32)
        from_high = k + (z <= k).astype(jnp.int32)
        far.append(jnp.where(z < nz // 2, from_low, from_high))
    near = far[:1] + far[:0:-1]

    def peer_z(step):
        return far[step] * ny + y

    def peer_y(step):
        return z * ny + lax.rem(y + step, ny)

    def src_at(zstep, ystep):
        return near[zstep] * ny + lax.rem(y + ystep, ny)

    def w_copy(layer):
        return pltpu.make_async_copy(w_ref.at[layer], w_v.at[layer], w_sem.at[layer])

    def top_copy(m, k):
        return pltpu.make_async_copy(
            top_ref.at[pl.ds(pl.multiple_of(m * rows, rows), rows), pl.ds(k * width, width)],
            buf_u.at[m, k], recv_u.at[m, k])

    def remote(src, dst, ssem, rsem, to_sec, to_tp):
        return pltpu.make_async_remote_copy(
            src_ref=src, dst_ref=dst, send_sem=ssem, recv_sem=rsem,
            device_id=(to_sec, to_tp), device_id_type=MESH)

    rank_in, rank_out = ib_ref.shape[1], ob_ref.shape[1]

    def prepare_bases():
        gap_in = jnp.zeros((rank_in, width), jnp.float32)
        gap_out = jnp.zeros((EXAMPLES * rank_out, width), jnp.float32)
        for layer in range(2):
            basis_in = ib_ref[layer].astype(jnp.float32)
            basis_out = [ob_ref[layer].astype(jnp.float32)] * EXAMPLES
            ins = [basis_in, gap_in] if layer == 0 else [gap_in, basis_in]
            outs = basis_out + [gap_out] if layer == 0 else [gap_out] + basis_out
            ib_v[layer] = jnp.concatenate(ins, 0).astype(jnp.bfloat16)
            ob_v[layer] = jnp.concatenate(outs, 0).astype(jnp.bfloat16)

    @pl.when(is_top)
    def _():
        @pl.loop(0, micro)
        def _(m):
            for k in range(tp_count):
                top_copy(m, k).start()

    w_copy(1).start()
    w_copy(0).start()

    barrier = pltpu.get_barrier_semaphore()

    def greet(to_sec, to_tp):
        pl.semaphore_signal(barrier, inc=1, device_id=(to_sec, to_tp), device_id_type=MESH)

    for step in range(1, tp_count):
        greet(sec, lax.rem(tp + step, tp_count))

    @pl.when(has_lower)
    def _():
        for step in range(nz):
            greet(sec - 1, peer_z(step))

    @pl.when(jnp.logical_not(is_top))
    def _():
        for step in range(nz):
            greet(sec + 1, peer_z(step))

    for step in range(1, sections):
        other = lax.rem(sec + step, sections)

        @pl.when(jnp.logical_and(other != sec + 1, other != sec - 1))
        def _(other=other):
            greet(other, tp)

    prepare_bases()
    linked = has_lower.astype(jnp.int32) + jnp.logical_not(is_top).astype(jnp.int32)
    pl.semaphore_wait(barrier, tp_count + sections - 2 + (nz - 1) * linked)

    def relay_u_copy(m, zstep, ystep):
        src = src_at(zstep, 0)
        return remote(buf_u.at[m, src], buf_u.at[m, src], relay_u.at[m, zstep, ystep],
                      recv_u.at[m, src], sec, peer_y(ystep))

    def relay_m_copy(m, zstep, ystep):
        src = src_at(zstep, 0)
        return remote(buf_m.at[m, src], buf_m.at[m, src], relay_m.at[m, zstep, ystep],
                      recv_m.at[m, src], sec, peer_y(ystep))

    def middle_copy(m, zstep):
        return remote(buf_m.at[m, tp], buf_m.at[m, tp], send_m.at[m, zstep],
                      recv_m.at[m, tp], sec, peer_z(zstep))

    def lower_copy(m, zstep):
        return remote(buf_l.at[m], buf_u.at[m, tp], send_l.at[m, zstep],
                      recv_u.at[m, tp], sec - 1, peer_z(zstep))

    def await_u(m, src):
        remote(buf_u.at[m, src], buf_u.at[m, src], send_my, recv_u.at[m, src], sec, tp).wait_recv()

    def await_m(m, src):
        remote(buf_m.at[m, src], buf_m.at[m, src], send_my, recv_m.at[m, src], sec, tp).wait_recv()

    def product(buf, m, layer, ystep, total=None):
        for zstep in range(nz):
            src = src_at(zstep, ystep)
            columns = pl.ds(pl.multiple_of(src * width, width), width)
            term = lax.dot_general(
                buf[m, src], w_v[layer, :, columns], NT, preferred_element_type=jnp.float32)
            total = term if total is None else total + term
        return total

    def upper(m):
        at = pl.ds(pl.multiple_of(m * rows, rows), rows)
        own = buf_u[m, tp]
        floats = own.astype(jnp.float32)
        slope = slope_of(h_ref[1, at, :])
        total = product(buf_u, m, 1, 0)
        for ystep in range(1, ny):
            @pl.when(jnp.logical_not(is_top))
            def _(ystep=ystep):
                for zstep in range(nz):
                    await_u(m, src_at(zstep, ystep))

            total = product(buf_u, m, 1, ystep, total)
        middle = (floats + slope * total).astype(jnp.bfloat16)
        buf_m[m, tp] = middle

        @pl.when(has_lower)
        def _():
            for step in range(1, nz):
                middle_copy(m, step).start()
            for step in range(1, ny):
                relay_m_copy(m, 0, step).start()

        feats = lax.dot_general(
            own, ob_v[1], NT, preferred_element_type=jnp.float32
        ) + lax.dot_general(middle, ob_v[0], NT, preferred_element_type=jnp.float32)
        example = se_ref[m * rows // (micro * rows // se_ref.shape[0])]
        lane_example = lax.rem(
            lax.broadcasted_iota(jnp.int32, feats.shape, 1) // rank_out, EXAMPLES)
        out_v[at, :] = jnp.where(lane_example == example, feats, 0.0)

    def lower(m):
        at = pl.ds(pl.multiple_of(m * rows, rows), rows)
        floats = buf_m[m, tp].astype(jnp.float32)
        slope = slope_of(h_ref[0, at, :])
        total = product(buf_m, m, 0, 0)
        for ystep in range(1, ny):
            for zstep in range(nz):
                await_m(m, src_at(zstep, ystep))
            total = product(buf_m, m, 0, ystep, total)
        buf_l[m] = (floats + slope * total).astype(jnp.bfloat16)
        for step in [*range(1, nz), 0]:
            lower_copy(m, step).start()

    def tp_copy(src, dst, ssem, rsem, to_tp):
        return remote(src, dst, ssem, rsem, sec, to_tp)

    def part_copy(step):
        to = lax.rem(tp + step, tp_count)
        return tp_copy(part_in.at[to], got_in.at[tp], part_send.at[step], part_recv.at[tp], to)

    def full_copy(step):
        to = lax.rem(tp + step, tp_count)
        return tp_copy(full_in.at[tp], full_in.at[tp], full_send.at[step], full_recv.at[tp], to)

    def grad_copy(step):
        to = lax.rem(tp + step, tp_count)
        return tp_copy(grad_v.at[tp], grad_v.at[tp], grad_send.at[step], grad_recv.at[tp], to)

    def score_copy(step):
        to = lax.rem(sec + step, sections)
        return remote(score_v.at[sec], score_v.at[sec], score_send.at[step],
                      score_recv.at[sec], to, tp)

    def project_inputs():
        part_rows = part_in.shape[1]

        @pl.loop(0, tp_count)
        def _(k):
            at = pl.ds(pl.multiple_of(k * part_rows, part_rows), part_rows)
            total = None
            for layer in range(2):
                floats = h_ref[layer, at, :].astype(jnp.float32)
                activated = (floats * jax.nn.sigmoid(floats)).astype(jnp.bfloat16)
                term = lax.dot_general(
                    activated, ib_v[layer], NT, preferred_element_type=jnp.float32)
                total = term if total is None else total + term
            part_in[k] = total

        for step in range(1, tp_count):
            part_copy(step).start()
        total = part_in[tp]
        for step in range(1, tp_count):
            src = lax.rem(tp + step, tp_count)
            tp_copy(got_in.at[src], got_in.at[src], send_my, part_recv.at[src], tp).wait_recv()
            total = total + got_in[src]
        full_in[tp] = total
        for step in range(1, tp_count):
            full_copy(step).start()

    @pl.when(sec < sections // 2)
    def _():
        project_inputs()

    def pass_middle(m):
        for zstep in range(1, nz):
            await_m(m, src_at(zstep, 0))
            for ystep in range(1, ny):
                relay_m_copy(m, zstep, ystep).start()

    @pl.loop(0, micro + 2)
    def _(it):
        with_middle = jnp.logical_and(jnp.logical_and(it >= 1, it <= micro), has_lower)
        lag = is_top.astype(jnp.int32)
        m_low = it - 1 - lag
        with_lower = jnp.logical_and(jnp.logical_and(m_low >= 0, m_low < micro), has_lower)

        @pl.when(jnp.logical_and(it < micro, jnp.logical_not(is_top)))
        def _():
            for zstep in range(nz):
                await_u(it, src_at(zstep, 0))
                for ystep in range(1, ny):
                    relay_u_copy(it, zstep, ystep).start()

        @pl.when(jnp.logical_and(with_middle, jnp.logical_not(is_top)))
        def _():
            pass_middle(it - 1)

        @pl.when(it == 0)
        def _():
            w_copy(1).wait()

        @pl.when(it == 1)
        def _():
            w_copy(0).wait()

        @pl.when(it < micro)
        def _():
            @pl.when(is_top)
            def _():
                for k in range(tp_count):
                    top_copy(it, k).wait()

            upper(it)

        @pl.when(jnp.logical_and(with_middle, is_top))
        def _():
            pass_middle(it - 1)

        @pl.when(with_lower)
        def _():
            lower(m_low)

    @pl.when(sec >= sections // 2)
    def _():
        project_inputs()

    for step in range(1, tp_count):
        src = lax.rem(tp + step, tp_count)
        tp_copy(full_in.at[src], full_in.at[src], send_my, full_recv.at[src], tp).wait_recv()
    lanes = 2 * rank_in
    pairs = EXAMPLES * rank_out
    product_all = lax.dot_general(
        out_v[...], full_in[...].reshape(micro * rows, lanes), (((0,), (0,)), ((), ())),
        precision=lax.Precision.HIGHEST, preferred_element_type=jnp.float32)
    lane = lax.broadcasted_iota(jnp.int32, (pairs, lanes), 1)
    grad_v[tp] = jnp.where(lane < rank_in, product_all[:pairs], product_all[pairs:])
    for step in range(1, tp_count):
        grad_copy(step).start()
    for step in range(1, tp_count):
        src = lax.rem(tp + step, tp_count)
        tp_copy(grad_v.at[src], grad_v.at[src], send_my, grad_recv.at[src], tp).wait_recv()
    total = grad_v[0]
    for k in range(1, tp_count):
        total = total + grad_v[k]
    sum_v[...] = total
    half = rank_out // 2
    number = q_ref.shape[1]
    sums = []
    for example in range(EXAMPLES):
        even = sum_v[pl.ds(example * rank_out, half, stride=2), :]
        odd = sum_v[pl.ds(example * rank_out + 1, half, stride=2), :]
        acc = jnp.zeros((number, lanes), jnp.float32)
        for layer in range(2):
            part = slice(layer * rank_in, (layer + 1) * rank_in)
            tiles = jnp.concatenate([even[:, part], odd[:, part]], 1)
            for j in range(half):
                block = q_ref[layer, :, j * lanes:(j + 1) * lanes].astype(jnp.float32)
                acc = acc + tiles[j:j + 1, :] * block
        sums.append(acc)
    score_v[sec] = lax.dot_general(
        jnp.ones((8, lanes), jnp.float32), jnp.concatenate(sums, 0), NT,
        precision=lax.Precision.HIGHEST, preferred_element_type=jnp.float32)
    for step in range(1, sections):
        score_copy(step).start()
    for step in range(1, sections):
        src = lax.rem(sec + step, sections)
        remote(score_v.at[src], score_v.at[src], send_my, score_recv.at[src], sec, tp).wait_recv()
    total = score_v[0]
    for k in range(1, sections):
        total = total + score_v[k]
    for example in range(EXAMPLES):
        score_ref[example:example + 1, :] = total[0:1, example * number:(example + 1) * number]

    for step in range(1, tp_count):
        part_copy(step).wait_send()
        full_copy(step).wait_send()
        grad_copy(step).wait_send()
    for step in range(1, sections):
        score_copy(step).wait_send()

    @pl.loop(0, micro)
    def _(m):
        @pl.when(jnp.logical_not(is_top))
        def _():
            for zstep in range(nz):
                for ystep in range(1, ny):
                    relay_u_copy(m, zstep, ystep).wait_send()

        @pl.when(has_lower)
        def _():
            for zstep in range(1, nz):
                middle_copy(m, zstep).wait_send()
            for zstep in range(nz):
                for ystep in range(1, ny):
                    relay_m_copy(m, zstep, ystep).wait_send()
                lower_copy(m, zstep).wait_send()


def shards(
    layer_inputs, weights, input_basis, output_basis, queries, top_cotangent, sequence_example
):
    sections = lax.axis_size("section")
    tp_count = lax.axis_size("tp")
    tokens, width = layer_inputs.shape[1:]
    micro = tp_count
    rows = tokens // micro
    nz, ny = grid_of(tp_count)
    lanes = 2 * input_basis.shape[2]
    pairs = EXAMPLES * output_basis.shape[2]
    number = queries.shape[1]
    dma = pltpu.SemaphoreType.DMA
    vmem = pl.BlockSpec(memory_space=pltpu.VMEM)
    hbm = pl.BlockSpec(memory_space=pl.ANY)
    smem = pl.BlockSpec(memory_space=pltpu.SMEM)
    return pl.pallas_call(
        functools.partial(chain_kernel, sections, tp_count),
        out_shape=jax.ShapeDtypeStruct((EXAMPLES, number), jnp.float32),
        in_specs=[hbm, hbm, vmem, vmem, vmem, vmem, smem],
        out_specs=vmem,
        scratch_shapes=[
            pltpu.VMEM((micro, tp_count, rows, width), jnp.bfloat16),
            pltpu.VMEM((micro, tp_count, rows, width), jnp.bfloat16),
            pltpu.VMEM((micro, rows, width), jnp.bfloat16),
            pltpu.VMEM(weights.shape, jnp.bfloat16),
            pltpu.VMEM((2, 2 * pairs, width), jnp.bfloat16),
            pltpu.VMEM((2, lanes, width), jnp.bfloat16),
            pltpu.VMEM((tokens, 2 * pairs), jnp.float32),
            pltpu.VMEM((tp_count, tokens // tp_count, lanes), jnp.float32),
            pltpu.VMEM((tp_count, tokens // tp_count, lanes), jnp.float32),
            pltpu.VMEM((tp_count, tokens // tp_count, lanes), jnp.float32),
            pltpu.VMEM((tp_count, pairs, lanes), jnp.float32),
            pltpu.VMEM((pairs, lanes), jnp.float32),
            pltpu.VMEM((sections, 8, EXAMPLES * number), jnp.float32),
            dma((2,)),
            dma((micro, tp_count)),
            dma((micro, tp_count)),
            dma((micro, nz)),
            dma,
            dma((micro, nz, ny)),
            dma((micro, nz, ny)),
            dma((micro, nz)),
            dma((tp_count,)),
            dma((tp_count,)),
            dma((tp_count,)),
            dma((tp_count,)),
            dma((tp_count,)),
            dma((tp_count,)),
            dma((sections,)),
            dma((sections,)),
        ],
        compiler_params=pltpu.CompilerParams(
            collective_id=0, has_side_effects=True, vmem_limit_bytes=56 * 2**20),
    )(
        top_cotangent, weights, layer_inputs, jnp.swapaxes(input_basis, 1, 2),
        jnp.swapaxes(output_basis, 1, 2), queries, sequence_example)


def solution(mesh):
    placed = (
        P("section", None, "tp"),
        P("section", "tp", None),
        P("section", "tp", None),
        P("section", "tp", None),
        P("section", "tp", None),
        P(),
        P(),
    )
    return jax.shard_map(
        shards, mesh=mesh, in_specs=placed, out_specs=P(None, "tp"), check_vma=False
    )
```

```python
import functools

import jax
import jax.numpy as jnp
from jax import lax
from jax.experimental import pallas as pl
from jax.experimental.pallas import tpu as pltpu
from jax.sharding import PartitionSpec as P

EXAMPLES = 2
AHEAD = 4
MESH = pl.DeviceIdType.MESH
NT = (((1,), (1,)), ((), ()))


def grid_of(tp_count):
    ny = 1
    while (2 * ny) * (2 * ny) <= tp_count:
        ny *= 2
    return tp_count // ny, ny


def slope_of(hidden):
    floats = hidden.astype(jnp.float32)
    logistic = jax.nn.sigmoid(floats)
    return logistic * (1.0 + floats * (1.0 - logistic))


def chain_kernel(
    sections, tp_count, top_ref, w_ref, h_ref, ib_ref, ob_ref, q_ref, se_ref, score_ref,
    buf_u, buf_m, buf_l, w_v, ob_v, ib_v, out_v, part_in, got_in, full_in, grad_v, sum_v, score_v,
    w_sem, recv_u, recv_m, send_m, send_my, relay_u, relay_m, send_l,
    part_send, part_recv, full_send, full_recv, grad_send, grad_recv, score_send, score_recv, credit,
):
    nz, ny = grid_of(tp_count)
    sec = lax.axis_index("section")
    tp = lax.axis_index("tp")
    z, y = tp // ny, lax.rem(tp, ny)
    micro, _, rows, width = buf_u.shape
    is_top = sec == sections - 1
    has_lower = sec > 0

    far = [z]
    for k in range(nz - 1):
        down = nz - 1 - k
        from_low = down - (z >= down).astype(jnp.int32)
        from_high = k + (z <= k).astype(jnp.int32)
        far.append(jnp.where(z < nz // 2, from_low, from_high))
    near = far[:1] + far[:0:-1]

    def peer_z(step):
        return far[step] * ny + y

    def peer_y(step):
        return z * ny + lax.rem(y + step, ny)

    def src_at(zstep, ystep):
        return near[zstep] * ny + lax.rem(y + ystep, ny)

    def w_copy(layer):
        return pltpu.make_async_copy(w_ref.at[layer], w_v.at[layer], w_sem.at[layer])

    def top_copy(m, k):
        return pltpu.make_async_copy(
            top_ref.at[pl.ds(pl.multiple_of(m * rows, rows), rows), pl.ds(k * width, width)],
            buf_u.at[m, k], recv_u.at[m, k])

    def remote(src, dst, ssem, rsem, to_sec, to_tp):
        return pltpu.make_async_remote_copy(
            src_ref=src, dst_ref=dst, send_sem=ssem, recv_sem=rsem,
            device_id=(to_sec, to_tp), device_id_type=MESH)

    rank_in, rank_out = ib_ref.shape[1], ob_ref.shape[1]

    def prepare_bases():
        gap_in = jnp.zeros((rank_in, width), jnp.float32)
        gap_out = jnp.zeros((EXAMPLES * rank_out, width), jnp.float32)
        for layer in range(2):
            basis_in = ib_ref[layer].astype(jnp.float32)
            basis_out = [ob_ref[layer].astype(jnp.float32)] * EXAMPLES
            ins = [basis_in, gap_in] if layer == 0 else [gap_in, basis_in]
            outs = basis_out + [gap_out] if layer == 0 else [gap_out] + basis_out
            ib_v[layer] = jnp.concatenate(ins, 0).astype(jnp.bfloat16)
            ob_v[layer] = jnp.concatenate(outs, 0).astype(jnp.bfloat16)

    @pl.when(is_top)
    def _():
        @pl.loop(0, micro)
        def _(m):
            for k in range(tp_count):
                top_copy(m, k).start()

    w_copy(1).start()
    w_copy(0).start()

    barrier = pltpu.get_barrier_semaphore()

    def greet(to_sec, to_tp):
        pl.semaphore_signal(barrier, inc=1, device_id=(to_sec, to_tp), device_id_type=MESH)

    for step in range(1, tp_count):
        greet(sec, lax.rem(tp + step, tp_count))

    @pl.when(has_lower)
    def _():
        for step in range(nz):
            greet(sec - 1, peer_z(step))

    @pl.when(jnp.logical_not(is_top))
    def _():
        for step in range(nz):
            greet(sec + 1, peer_z(step))

    for step in range(1, sections):
        other = lax.rem(sec + step, sections)

        @pl.when(jnp.logical_and(other != sec + 1, other != sec - 1))
        def _(other=other):
            greet(other, tp)

    prepare_bases()
    linked = has_lower.astype(jnp.int32) + jnp.logical_not(is_top).astype(jnp.int32)
    pl.semaphore_wait(barrier, tp_count + sections - 2 + (nz - 1) * linked)

    def relay_u_copy(m, zstep, ystep):
        src = src_at(zstep, 0)
        return remote(buf_u.at[m, src], buf_u.at[m, src], relay_u.at[m, zstep, ystep],
                      recv_u.at[m, src], sec, peer_y(ystep))

    def relay_m_copy(m, zstep, ystep):
        src = src_at(zstep, 0)
        return remote(buf_m.at[m, src], buf_m.at[m, src], relay_m.at[m, zstep, ystep],
                      recv_m.at[m, src], sec, peer_y(ystep))

    def middle_copy(m, zstep):
        return remote(buf_m.at[m, tp], buf_m.at[m, tp], send_m.at[m, zstep],
                      recv_m.at[m, tp], sec, peer_z(zstep))

    def lower_copy(m, zstep):
        return remote(buf_l.at[m], buf_u.at[m, tp], send_l.at[m, zstep],
                      recv_u.at[m, tp], sec - 1, peer_z(zstep))

    def await_u(m, src):
        remote(buf_u.at[m, src], buf_u.at[m, src], send_my, recv_u.at[m, src], sec, tp).wait_recv()

    def await_m(m, src):
        remote(buf_m.at[m, src], buf_m.at[m, src], send_my, recv_m.at[m, src], sec, tp).wait_recv()

    def product(buf, m, layer, ystep, total=None):
        for zstep in range(nz):
            src = src_at(zstep, ystep)
            columns = pl.ds(pl.multiple_of(src * width, width), width)
            term = lax.dot_general(
                buf[m, src], w_v[layer, :, columns], NT, preferred_element_type=jnp.float32)
            total = term if total is None else total + term
        return total

    def upper(m):
        at = pl.ds(pl.multiple_of(m * rows, rows), rows)
        own = buf_u[m, tp]
        floats = own.astype(jnp.float32)
        slope = slope_of(h_ref[1, at, :])
        total = product(buf_u, m, 1, 0)
        for ystep in range(1, ny):
            @pl.when(jnp.logical_not(is_top))
            def _(ystep=ystep):
                for zstep in range(nz):
                    await_u(m, src_at(zstep, ystep))

            total = product(buf_u, m, 1, ystep, total)
        middle = (floats + slope * total).astype(jnp.bfloat16)
        buf_m[m, tp] = middle

        @pl.when(has_lower)
        def _():
            for step in range(1, nz):
                middle_copy(m, step).start()
            for step in range(1, ny):
                relay_m_copy(m, 0, step).start()

        feats = lax.dot_general(
            own, ob_v[1], NT, preferred_element_type=jnp.float32
        ) + lax.dot_general(middle, ob_v[0], NT, preferred_element_type=jnp.float32)
        example = se_ref[m * rows // (micro * rows // se_ref.shape[0])]
        lane_example = lax.rem(
            lax.broadcasted_iota(jnp.int32, feats.shape, 1) // rank_out, EXAMPLES)
        out_v[at, :] = jnp.where(lane_example == example, feats, 0.0)

    def lower(m):
        at = pl.ds(pl.multiple_of(m * rows, rows), rows)
        floats = buf_m[m, tp].astype(jnp.float32)
        slope = slope_of(h_ref[0, at, :])
        total = product(buf_m, m, 0, 0)
        for ystep in range(1, ny):
            for zstep in range(nz):
                await_m(m, src_at(zstep, ystep))
            total = product(buf_m, m, 0, ystep, total)
        buf_l[m] = (floats + slope * total).astype(jnp.bfloat16)
        for step in [*range(1, nz), 0]:
            lower_copy(m, step).start()

    def tp_copy(src, dst, ssem, rsem, to_tp):
        return remote(src, dst, ssem, rsem, sec, to_tp)

    def part_copy(step):
        to = lax.rem(tp + step, tp_count)
        return tp_copy(part_in.at[to], got_in.at[tp], part_send.at[step], part_recv.at[tp], to)

    def full_copy(step):
        to = lax.rem(tp + step, tp_count)
        return tp_copy(full_in.at[tp], full_in.at[tp], full_send.at[step], full_recv.at[tp], to)

    def grad_copy(step):
        to = lax.rem(tp + step, tp_count)
        return tp_copy(grad_v.at[tp], grad_v.at[tp], grad_send.at[step], grad_recv.at[tp], to)

    def score_copy(step):
        to = lax.rem(sec + step, sections)
        return remote(score_v.at[sec], score_v.at[sec], score_send.at[step],
                      score_recv.at[sec], to, tp)

    def project_inputs():
        part_rows = part_in.shape[1]

        @pl.loop(0, tp_count)
        def _(k):
            at = pl.ds(pl.multiple_of(k * part_rows, part_rows), part_rows)
            total = None
            for layer in range(2):
                floats = h_ref[layer, at, :].astype(jnp.float32)
                activated = (floats * jax.nn.sigmoid(floats)).astype(jnp.bfloat16)
                term = lax.dot_general(
                    activated, ib_v[layer], NT, preferred_element_type=jnp.float32)
                total = term if total is None else total + term
            part_in[k] = total

        for step in range(1, tp_count):
            part_copy(step).start()
        total = part_in[tp]
        for step in range(1, tp_count):
            src = lax.rem(tp + step, tp_count)
            tp_copy(got_in.at[src], got_in.at[src], send_my, part_recv.at[src], tp).wait_recv()
            total = total + got_in[src]
        full_in[tp] = total
        for step in range(1, tp_count):
            full_copy(step).start()

    @pl.when(sec < sections // 2)
    def _():
        project_inputs()

    def pass_middle(m):
        for zstep in range(1, nz):
            await_m(m, src_at(zstep, 0))
            for ystep in range(1, ny):
                relay_m_copy(m, zstep, ystep).start()

    @pl.loop(0, micro + 2)
    def _(it):
        with_middle = jnp.logical_and(jnp.logical_and(it >= 1, it <= micro), has_lower)
        lag = is_top.astype(jnp.int32)
        m_low = it - 1 - lag
        with_lower = jnp.logical_and(jnp.logical_and(m_low >= 0, m_low < micro), has_lower)

        @pl.when(jnp.logical_and(it < micro, jnp.logical_not(is_top)))
        def _():
            for zstep in range(nz):
                await_u(it, src_at(zstep, 0))
                for ystep in range(1, ny):
                    relay_u_copy(it, zstep, ystep).start()

        @pl.when(jnp.logical_and(with_middle, jnp.logical_not(is_top)))
        def _():
            pass_middle(it - 1)

        @pl.when(it == 0)
        def _():
            w_copy(1).wait()

        @pl.when(it == 1)
        def _():
            w_copy(0).wait()

        @pl.when(it < micro)
        def _():
            @pl.when(is_top)
            def _():
                for k in range(tp_count):
                    top_copy(it, k).wait()

            @pl.when(jnp.logical_and(is_top, it >= AHEAD))
            def _():
                pl.semaphore_wait(credit, 1)

            upper(it)

            @pl.when(sec == sections - 2)
            def _():
                pl.semaphore_signal(
                    credit, inc=1, device_id=(sec + 1, tp), device_id_type=MESH)

        @pl.when(jnp.logical_and(with_middle, is_top))
        def _():
            pass_middle(it - 1)

        @pl.when(with_lower)
        def _():
            lower(m_low)

    @pl.when(sec >= sections // 2)
    def _():
        project_inputs()

    for step in range(1, tp_count):
        src = lax.rem(tp + step, tp_count)
        tp_copy(full_in.at[src], full_in.at[src], send_my, full_recv.at[src], tp).wait_recv()
    lanes = 2 * rank_in
    pairs = EXAMPLES * rank_out
    product_all = lax.dot_general(
        out_v[...], full_in[...].reshape(micro * rows, lanes), (((0,), (0,)), ((), ())),
        precision=lax.Precision.HIGHEST, preferred_element_type=jnp.float32)
    lane = lax.broadcasted_iota(jnp.int32, (pairs, lanes), 1)
    grad_v[tp] = jnp.where(lane < rank_in, product_all[:pairs], product_all[pairs:])
    for step in range(1, tp_count):
        grad_copy(step).start()
    for step in range(1, tp_count):
        src = lax.rem(tp + step, tp_count)
        tp_copy(grad_v.at[src], grad_v.at[src], send_my, grad_recv.at[src], tp).wait_recv()
    total = grad_v[0]
    for k in range(1, tp_count):
        total = total + grad_v[k]
    sum_v[...] = total
    half = rank_out // 2
    number = q_ref.shape[1]
    sums = []
    for example in range(EXAMPLES):
        even = sum_v[pl.ds(example * rank_out, half, stride=2), :]
        odd = sum_v[pl.ds(example * rank_out + 1, half, stride=2), :]
        acc = jnp.zeros((number, lanes), jnp.float32)
        for layer in range(2):
            part = slice(layer * rank_in, (layer + 1) * rank_in)
            tiles = jnp.concatenate([even[:, part], odd[:, part]], 1)
            for j in range(half):
                block = q_ref[layer, :, j * lanes:(j + 1) * lanes].astype(jnp.float32)
                acc = acc + tiles[j:j + 1, :] * block
        sums.append(acc)
    score_v[sec] = lax.dot_general(
        jnp.ones((8, lanes), jnp.float32), jnp.concatenate(sums, 0), NT,
        precision=lax.Precision.HIGHEST, preferred_element_type=jnp.float32)
    for step in range(1, sections):
        score_copy(step).start()
    for step in range(1, sections):
        src = lax.rem(sec + step, sections)
        remote(score_v.at[src], score_v.at[src], send_my, score_recv.at[src], sec, tp).wait_recv()
    total = score_v[0]
    for k in range(1, sections):
        total = total + score_v[k]
    for example in range(EXAMPLES):
        score_ref[example:example + 1, :] = total[0:1, example * number:(example + 1) * number]

    @pl.when(is_top)
    def _():
        pl.semaphore_wait(credit, min(AHEAD, micro))

    for step in range(1, tp_count):
        part_copy(step).wait_send()
        full_copy(step).wait_send()
        grad_copy(step).wait_send()
    for step in range(1, sections):
        score_copy(step).wait_send()

    @pl.loop(0, micro)
    def _(m):
        @pl.when(jnp.logical_not(is_top))
        def _():
            for zstep in range(nz):
                for ystep in range(1, ny):
                    relay_u_copy(m, zstep, ystep).wait_send()

        @pl.when(has_lower)
        def _():
            for zstep in range(1, nz):
                middle_copy(m, zstep).wait_send()
            for zstep in range(nz):
                for ystep in range(1, ny):
                    relay_m_copy(m, zstep, ystep).wait_send()
                lower_copy(m, zstep).wait_send()


def shards(
    layer_inputs, weights, input_basis, output_basis, queries, top_cotangent, sequence_example
):
    sections = lax.axis_size("section")
    tp_count = lax.axis_size("tp")
    tokens, width = layer_inputs.shape[1:]
    micro = tp_count
    rows = tokens // micro
    nz, ny = grid_of(tp_count)
    lanes = 2 * input_basis.shape[2]
    pairs = EXAMPLES * output_basis.shape[2]
    number = queries.shape[1]
    dma = pltpu.SemaphoreType.DMA
    vmem = pl.BlockSpec(memory_space=pltpu.VMEM)
    hbm = pl.BlockSpec(memory_space=pl.ANY)
    smem = pl.BlockSpec(memory_space=pltpu.SMEM)
    return pl.pallas_call(
        functools.partial(chain_kernel, sections, tp_count),
        out_shape=jax.ShapeDtypeStruct((EXAMPLES, number), jnp.float32),
        in_specs=[hbm, hbm, vmem, vmem, vmem, vmem, smem],
        out_specs=vmem,
        scratch_shapes=[
            pltpu.VMEM((micro, tp_count, rows, width), jnp.bfloat16),
            pltpu.VMEM((micro, tp_count, rows, width), jnp.bfloat16),
            pltpu.VMEM((micro, rows, width), jnp.bfloat16),
            pltpu.VMEM(weights.shape, jnp.bfloat16),
            pltpu.VMEM((2, 2 * pairs, width), jnp.bfloat16),
            pltpu.VMEM((2, lanes, width), jnp.bfloat16),
            pltpu.VMEM((tokens, 2 * pairs), jnp.float32),
            pltpu.VMEM((tp_count, tokens // tp_count, lanes), jnp.float32),
            pltpu.VMEM((tp_count, tokens // tp_count, lanes), jnp.float32),
            pltpu.VMEM((tp_count, tokens // tp_count, lanes), jnp.float32),
            pltpu.VMEM((tp_count, pairs, lanes), jnp.float32),
            pltpu.VMEM((pairs, lanes), jnp.float32),
            pltpu.VMEM((sections, 8, EXAMPLES * number), jnp.float32),
            dma((2,)),
            dma((micro, tp_count)),
            dma((micro, tp_count)),
            dma((micro, nz)),
            dma,
            dma((micro, nz, ny)),
            dma((micro, nz, ny)),
            dma((micro, nz)),
            dma((tp_count,)),
            dma((tp_count,)),
            dma((tp_count,)),
            dma((tp_count,)),
            dma((tp_count,)),
            dma((tp_count,)),
            dma((sections,)),
            dma((sections,)),
            pltpu.SemaphoreType.REGULAR,
        ],
        compiler_params=pltpu.CompilerParams(
            collective_id=0, has_side_effects=True, vmem_limit_bytes=56 * 2**20),
    )(
        top_cotangent, weights, layer_inputs, jnp.swapaxes(input_basis, 1, 2),
        jnp.swapaxes(output_basis, 1, 2), queries, sequence_example)


def solution(mesh):
    placed = (
        P("section", None, "tp"),
        P("section", "tp", None),
        P("section", "tp", None),
        P("section", "tp", None),
        P("section", "tp", None),
        P(),
        P(),
    )
    return jax.shard_map(
        shards, mesh=mesh, in_specs=placed, out_specs=P(None, "tp"), check_vma=False
    )
```
